32 devices in a mesh: pb: 16 (over z, x, core), wa: 2 (over y).
Axes of the slice: x: 2, y: 2, z: 4, core: 2. Of those that a mesh axis runs over, the one named last changes fastest.
Arguments:
- psi_val: bfloat16 [16, 8, 1024], P('wa', None, 'pb'), may hold values from -0.796875 to 0.796875
- psi_cond: bfloat16 [16, 12, 1024], P('wa', None, 'pb'), may hold values from -0.796875 to 0.796875
- trials: bfloat16 [16, 1536], P('wa', 'pb'), may hold values from -6 to 6
- screened: bfloat16 [16, 1024, 1024], P('pb', 'wa'), may hold values from -0.1875 to 0.1875
- kmap: int32 [16, 16], P('pb'), may hold values from 0 to 15, each once within a row
Outputs:
- action: float32 [16, 1536], P('wa', 'pb')
The draws below stay inside these ranges and needn't reach their ends.
Inputs may be any that keep to these rules, and one draw needn't show every extreme that they name: Every row of kmap is a permutation of the 16 k-points.
All inputs are finite; a program needn't handle non-finite values.
Results may differ from the reference program's by a relative error of at most 0.005.
Values may be sent and summed in bfloat16 or wider, within the bound.
A program may use at most 64 MiB of HBM per device.

```python
import jax
import jax.numpy as jnp
from jax import lax

V = 8
C = 12
MU = 1024
K = 16
S = 16
Q = 16


def level_of(stream_key, shape, split, smallest, top_value):
    loudness = 1.0
    for position, shards_of in split:
        steps = jax.random.uniform(jax.random.fold_in(jax.random.fold_in(stream_key, 6), position), (shards_of,), jnp.float32, smallest / len(split), top_value / len(split))
        loudness = loudness * jnp.repeat(jnp.exp(steps), shape[position] // shards_of).reshape((-1,) + (1,) * (len(shape) - 1 - position))
    return loudness


def gaussian(key, dims, scale, bound, shards=(), held_as=jnp.bfloat16):
    values = scale * jax.random.normal(key, dims, jnp.float32)
    if shards:
        values = values * level_of(key, dims, shards, -0.22, 0.18)
    return jnp.clip(values, -bound, bound).astype(held_as)


def setup_inputs(seed: int = 0) -> dict:
    streams_of = jax.random.split(jax.random.key(seed), 6)
    psi_val = gaussian(streams_of[0], (K, V, MU), 0.13, 0.796875, ((0, 2), (2, 16)))
    psi_cond = gaussian(streams_of[1], (K, C, MU), 0.13, 0.796875, ((0, 2), (2, 16)))
    trials = gaussian(streams_of[2], (K, S * V * C), 1.0, 6.0, ((0, 2), (1, 16)))
    screened = gaussian(streams_of[3], (Q, MU, MU), MU ** -0.5, 0.1875, ((0, 16), (1, 2)))
    kmap = jax.vmap(lambda own: jax.random.permutation(own, K))(jax.random.split(streams_of[4], Q)).reshape((Q, K)).astype(jnp.int32)
    return dict(psi_val=psi_val, psi_cond=psi_cond, trials=trials, screened=screened, kmap=kmap)


def one_transfer(psi_val, psi_cond, xfull, wq, row):
    hi = lax.Precision.HIGHEST
    valf = psi_val.astype(jnp.float32)
    condf = psi_cond.astype(jnp.float32)
    valp = valf[row]
    condp = condf[row]
    apair = (valf[:, :, None, :] * valp[:, None, :, :]).astype(jnp.bfloat16)
    bpair = (condf[:, :, None, :] * condp[:, None, :, :]).astype(jnp.bfloat16)
    wfull = wq.astype(jnp.float32)
    wa_term = jnp.dot(apair.reshape(-1, MU).astype(jnp.float32), wfull.T, precision=hi).astype(jnp.bfloat16)
    wb_term = jnp.dot(bpair.reshape(-1, MU).astype(jnp.float32), wfull.T, precision=hi).astype(jnp.bfloat16)
    wa_term = wa_term.reshape(K, V, V, MU).astype(jnp.float32)
    wb_term = wb_term.reshape(K, C, C, MU).astype(jnp.float32)
    gmat = jnp.einsum('kcdm,kvum->kcdvu', bpair.astype(jnp.float32), wa_term, precision=hi)
    hmat = jnp.einsum('kcdm,kvum->kcdvu', wb_term, apair.astype(jnp.float32), precision=hi)
    forward = jnp.einsum('kcdvu,ksud->ksvc', gmat, xfull[row], precision=hi)
    backward = jnp.einsum('kdcuv,ksud->ksvc', hmat, xfull, precision=hi)
    return forward + jnp.zeros((K, S, V, C), jnp.float32).at[row].add(backward)


def reference(psi_val, psi_cond, trials, screened, kmap):
    xfull = trials.astype(jnp.float32).reshape(K, S, V, C)

    def step(total, pieces):
        wq, row = pieces
        return total + one_transfer(psi_val, psi_cond, xfull, wq, row.astype(jnp.int32)), None

    total, unused = lax.scan(step, jnp.zeros((K, S, V, C), jnp.float32), (screened, kmap))
    return total.reshape(K, S * V * C)
```

```python
import functools
import math

import jax
import jax.numpy as jnp
from jax import lax
from jax.experimental import pallas as pl
from jax.experimental.pallas import tpu as pltpu
from jax.sharding import PartitionSpec as P

MESH = pl.DeviceIdType.MESH
LANES = 128
PACK = 16
F32 = jnp.float32
BF16 = jnp.bfloat16


def up(value, unit):
    return -(-value // unit) * unit


def gather_kernel(npb, nwa, x_ref, out_ref, own_sem, send_sem, recv_sem, fsend_sem, frecv_sem):
    pb, wa = lax.axis_index("pb"), lax.axis_index("wa")
    core = lax.rem(pb, 2)
    chip = (pb // 2) * nwa + wa
    nchips = npb // 2 * nwa

    def place(t, c):
        return (t // nwa) * 2 + c, lax.rem(t, nwa)

    barrier = pltpu.get_barrier_semaphore()
    pl.semaphore_signal(barrier, inc=1, device_id=place(chip, 1 - core), device_id_type=MESH)

    def greet(j, carry):
        t = lax.rem(chip + j, nchips)
        pl.semaphore_signal(barrier, inc=1, device_id=place(t, core), device_id_type=MESH)
        return carry

    lax.fori_loop(1, nchips, greet, 0)
    own = pltpu.make_async_copy(x_ref, out_ref.at[chip * 2 + core], own_sem)
    own.start()
    pl.semaphore_wait(barrier, nchips)

    def first(j):
        t = lax.rem(chip + j, nchips)
        return pltpu.make_async_remote_copy(
            src_ref=x_ref, dst_ref=out_ref.at[chip * 2 + core], send_sem=send_sem.at[j],
            recv_sem=recv_sem.at[j], device_id=place(t, core), device_id_type=MESH)

    def arrival(j):
        t = lax.rem(chip - j + nchips, nchips)
        return pltpu.make_async_remote_copy(
            src_ref=x_ref, dst_ref=out_ref.at[t * 2 + core], send_sem=send_sem.at[j],
            recv_sem=recv_sem.at[j], device_id=place(t, core), device_id_type=MESH)

    def second(j, source, c):
        t = lax.rem(chip - j + nchips, nchips)
        return pltpu.make_async_remote_copy(
            src_ref=source if source is not None else out_ref.at[t * 2 + core],
            dst_ref=out_ref.at[t * 2 + c], send_sem=fsend_sem.at[j],
            recv_sem=frecv_sem.at[j], device_id=place(chip, 1 - core), device_id_type=MESH)

    def send(j, carry):
        first(j).start()
        return carry

    lax.fori_loop(1, nchips, send, 0)
    second(0, x_ref, core).start()

    def forward(j, carry):
        arrival(j).wait_recv()
        second(j, None, core).start()
        return carry

    lax.fori_loop(1, nchips, forward, 0)

    def finish(j, carry):
        second(j, None, 1 - core).wait_recv()
        second(j, None, core).wait_send()
        return carry

    def finish_first(j, carry):
        first(j).wait_send()
        return carry

    lax.fori_loop(0, nchips, finish, 0)
    lax.fori_loop(1, nchips, finish_first, 0)
    own.wait()


def reduce_kernel(npb, nwa, x_ref, out_ref, slots, own_sem, send_sem, recv_sem):
    pb, wa = lax.axis_index("pb"), lax.axis_index("wa")
    me = pb * nwa + wa
    n = npb * nwa
    barrier = pltpu.get_barrier_semaphore()

    def place(t):
        return t // nwa, lax.rem(t, nwa)

    def greet(j, carry):
        pl.semaphore_signal(barrier, inc=1, device_id=place(lax.rem(me + j, n)), device_id_type=MESH)
        return carry

    lax.fori_loop(1, n, greet, 0)
    own = pltpu.make_async_copy(x_ref.at[me], slots.at[0], own_sem)
    own.start()
    pl.semaphore_wait(barrier, n - 1)

    def copy(j):
        t = lax.rem(me + j, n)
        return pltpu.make_async_remote_copy(
            src_ref=x_ref.at[t], dst_ref=slots.at[j], send_sem=send_sem.at[j],
            recv_sem=recv_sem.at[j], device_id=place(t), device_id_type=MESH)

    def send(j, carry):
        copy(j).start()
        return carry

    lax.fori_loop(1, n, send, 0)
    own.wait()

    def receive(j, carry):
        copy(j).wait_recv()
        return carry

    lax.fori_loop(1, n, receive, 0)
    total = slots[0]
    for j in range(1, n):
        total = total + slots[j]
    out_ref[...] = total

    def finish(j, carry):
        copy(j).wait_send()
        return carry

    lax.fori_loop(1, n, finish, 0)


def compute_kernel(dims, kmap_ref, inv_ref, val_ref, cond_ref, x_ref, w_ref, out_ref,
                   a_ref, wa_ref, aw_ref, y_ref, z_ref, acc_ref):
    kcount, nval, ncond, ntrial, points, nrows, nwa, npb = dims
    klocal = kcount // nwa
    crows = cond_ref.shape[1]
    row0 = pl.multiple_of(lax.axis_index("wa") * nrows, nrows)
    pairs = nval * nval
    block = math.gcd(kcount, max(1, 256 // pairs))

    def one_y(k, carry):
        y_ref[k] = lax.dot_general(x_ref[k], cond_ref[k], (((1,), (0,)), ((), ())), preferred_element_type=F32)
        return carry

    lax.fori_loop(0, kcount, one_y, 0)

    def build(b, index_ref, start, width):
        for i in range(block):
            k = b * block + i
            here = val_ref[k, :, pl.ds(start, width)]
            there = val_ref[index_ref[k], :, pl.ds(start, width)]
            for v in range(0, nval, 2):
                two = jnp.concatenate([here[v:v + 1] * there, here[v + 1:v + 2] * there], axis=0)
                a_ref[pl.ds(i * pairs + v * nval, 2 * nval), 0:width] = two.astype(BF16)

    def first(b, carry):
        build(b, kmap_ref, 0, points)
        out = lax.dot_general(a_ref[...], w_ref[...], (((1,), (1,)), ((), ())), preferred_element_type=F32)
        wa_ref[pl.ds(b * block, block)] = out.astype(BF16).astype(F32).reshape(block, pairs, nrows)
        return carry

    lax.fori_loop(0, kcount // block, first, 0)

    def second(b, carry):
        build(b, inv_ref, row0, nrows)
        out = lax.dot_general(a_ref[:, 0:nrows], w_ref[...], (((1,), (0,)), ((), ())), preferred_element_type=F32)
        aw_ref[pl.ds(b * block, block)] = out.reshape(block, pairs, points)
        return carry

    lax.fori_loop(0, kcount // block, second, 0)
    acc_ref[...] = jnp.zeros_like(acc_ref)
    chunk = math.gcd(nrows, LANES)

    def combine(k, weight_ref, other, start, base, width):
        for c in range(0, width, chunk):
            at = pl.ds(pl.multiple_of(start + c, chunk), chunk)
            ys = [y_ref[other, u * ntrial:(u + 1) * ntrial, at] for u in range(nval)]
            for v in range(nval):
                total = None
                for u in range(nval):
                    row = v * nval + u
                    term = weight_ref[k, row:row + 1, c:c + chunk] * ys[u]
                    total = term if total is None else total + term
                z_ref[v * ntrial:(v + 1) * ntrial, base + c:base + c + chunk] = total.astype(BF16)

    def one_k(k, carry):
        combine(k, wa_ref, kmap_ref[k], row0, 0, nrows)
        combine(k, aw_ref, inv_ref[k], 0, nrows, points)
        spot = lax.rem(k, klocal)
        both = jnp.concatenate([cond_ref[k, :, pl.ds(row0, nrows)], cond_ref[k]], axis=1)
        wide = jnp.concatenate(
            [both * jnp.where(spot == j, 1.0, 0.0).astype(BF16) for j in range(klocal)], axis=0)
        acc_ref[k // klocal] += lax.dot_general(
            z_ref[...], wide, (((1,), (1,)), ((), ())), preferred_element_type=F32)
        return carry

    lax.fori_loop(0, kcount, one_k, 0)
    r = out_ref.shape[1]
    for i in range(npb):
        s, v0 = i * r // nval, i * r % nval
        for w in range(nwa):
            out_ref[i * nwa + w] = acc_ref[w, pl.ds(v0 * ntrial + s, r, stride=ntrial), :]


def shards(npb, nwa, psi_val, psi_cond, trials, screened, kmap):
    klocal, nval, pts = psi_val.shape
    ncond = psi_cond.shape[1]
    cols = trials.shape[1]
    kcount, points = klocal * nwa, pts * npb
    ntrial = cols * npb // (nval * ncond)
    weights = screened[0]
    nrows = weights.shape[0]
    row = kmap[0]
    inverse = jnp.sum(
        jnp.where(row[None, :] == jnp.arange(kcount, dtype=jnp.int32)[:, None], jnp.arange(kcount, dtype=jnp.int32)[None, :], 0),
        axis=1).astype(jnp.int32)
    vmem = pl.BlockSpec(memory_space=pltpu.VMEM)
    smem = pl.BlockSpec(memory_space=pltpu.SMEM)

    flat = jnp.concatenate([psi_val.reshape(-1), psi_cond.reshape(-1), trials.reshape(-1)])
    size = flat.shape[0]
    rows = up(-(-size // LANES), PACK)
    packed = jnp.pad(flat, (0, rows * LANES - size)).reshape(rows, LANES)
    n = npb * nwa
    nchips = n // 2
    gathered = pl.pallas_call(
        functools.partial(gather_kernel, npb, nwa),
        out_shape=jax.ShapeDtypeStruct((n, rows, LANES), BF16),
        in_specs=[vmem], out_specs=vmem,
        scratch_shapes=[pltpu.SemaphoreType.DMA] + [pltpu.SemaphoreType.DMA((nchips,))] * 4,
        compiler_params=pltpu.CompilerParams(collective_id=0, has_side_effects=True),
        name="gather",
    )(packed)
    gathered = gathered.reshape(npb // 2, nwa, 2, rows * LANES)
    nv, nc = klocal * nval * pts, klocal * ncond * pts
    val = gathered[..., :nv].reshape(npb // 2, nwa, 2, klocal, nval, pts)
    cond = gathered[..., nv:nv + nc].reshape(npb // 2, nwa, 2, klocal, ncond, pts)
    tri = gathered[..., nv + nc:size].reshape(npb // 2, nwa, 2, klocal, cols)
    val = val.transpose(1, 3, 4, 0, 2, 5).reshape(kcount, nval, points).astype(F32)
    cond = cond.transpose(1, 3, 4, 0, 2, 5).reshape(kcount, ncond, points)
    crows = up(ncond, PACK)
    cond = jnp.pad(cond, ((0, 0), (0, crows - ncond), (0, 0)))
    tri = tri.transpose(1, 3, 0, 2, 4).reshape(kcount, ntrial, nval, ncond)
    tri = jnp.pad(tri.transpose(0, 2, 1, 3).reshape(kcount, nval * ntrial, ncond), ((0, 0), (0, 0), (0, crows - ncond)))

    r = cols // ncond
    width = klocal * crows
    pairs = nval * nval
    block = math.gcd(kcount, max(1, 256 // pairs))
    dims = (kcount, nval, ncond, ntrial, points, nrows, nwa, npb)
    partial = pl.pallas_call(
        functools.partial(compute_kernel, dims),
        out_shape=jax.ShapeDtypeStruct((n, r, width), F32),
        in_specs=[smem, smem, vmem, vmem, vmem, vmem], out_specs=vmem,
        scratch_shapes=[
            pltpu.VMEM((block * pairs, points), BF16),
            pltpu.VMEM((kcount, pairs, nrows), F32),
            pltpu.VMEM((kcount, pairs, points), F32),
            pltpu.VMEM((kcount, nval * ntrial, points), F32),
            pltpu.VMEM((nval * ntrial, nrows + points), BF16),
            pltpu.VMEM((nwa, nval * ntrial, width), F32),
        ],
        name="compute",
    )(row, inverse, val, cond, tri, weights)
    mine = pl.pallas_call(
        functools.partial(reduce_kernel, npb, nwa),
        out_shape=jax.ShapeDtypeStruct((r, width), F32),
        in_specs=[vmem], out_specs=vmem,
        scratch_shapes=[pltpu.VMEM((n, r, width), F32), pltpu.SemaphoreType.DMA] + [pltpu.SemaphoreType.DMA((n,))] * 2,
        compiler_params=pltpu.CompilerParams(collective_id=1, has_side_effects=True),
        name="reduce",
    )(partial)
    mine = mine.reshape(r, klocal, crows)[:, :, :ncond]
    return mine.transpose(1, 0, 2).reshape(klocal, cols)


def solution(mesh):
    in_specs = (
        P("wa", None, "pb"),
        P("wa", None, "pb"),
        P("wa", "pb"),
        P("pb", "wa", None),
        P("pb", None),
    )
    body = functools.partial(shards, mesh.shape["pb"], mesh.shape["wa"])
    return jax.shard_map(body, mesh=mesh, in_specs=in_specs, out_specs=P("wa", "pb"), check_vma=False)
```

```python
import functools
import math

import jax
import jax.numpy as jnp
from jax import lax
from jax.experimental import pallas as pl
from jax.experimental.pallas import tpu as pltpu
from jax.sharding import PartitionSpec as P

MESH = pl.DeviceIdType.MESH
LANES = 128
PACK = 16
F32 = jnp.float32
BF16 = jnp.bfloat16


def up(value, unit):
    return -(-value // unit) * unit


def kernel(dims, kmap_ref, x_ref, w_ref, out_ref, slots, val_ref, cond_ref, condb_ref, tri_ref,
           a_ref, wa_ref, aw_ref, y_ref, z_ref, acc_ref, part_ref, rslots,
           own_sem, send_sem, recv_sem, fsend_sem, frecv_sem, rsend_sem, rrecv_sem):
    npb, nwa, klocal, nval, ncond, pts, ntrial, nrows, g, r = dims
    kcount, points, n = klocal * nwa, pts * npb, npb * nwa
    crows = condb_ref.shape[1]
    pb, wa = lax.axis_index("pb"), lax.axis_index("wa")
    me = wa * npb + pb
    nx = 2 if npb % 4 == 0 else 1
    nz = npb // (2 * nx)
    core, px, pz = lax.rem(pb, 2), lax.rem(pb // 2, nx), pb // (2 * nx)

    def device(z, x, y, c):
        return (z * nx + x) * 2 + c, y

    def source(z, x, y):
        return (lax.rem(pz - z + nz, nz), lax.rem(px - x + nx, nx), lax.rem(wa - y + nwa, nwa))

    def target(z, x, y):
        return (lax.rem(pz + z, nz), lax.rem(px + x, nx), lax.rem(wa + y, nwa))

    def slot(z, x, y, c):
        p, w = device(z, x, y, c)
        return slots.at[w * npb + p]

    barrier = pltpu.get_barrier_semaphore()

    def greet(j, carry):
        t = lax.rem(me + j, n)
        pl.semaphore_signal(barrier, inc=1, device_id=(lax.rem(t, npb), t // npb), device_id_type=MESH)
        return carry

    lax.fori_loop(1, n, greet, 0)
    own = pltpu.make_async_copy(x_ref, slots.at[me], own_sem)
    own.start()
    pl.semaphore_wait(barrier, n - 1)

    def hop(z, x, y, last):
        held = (z if last != 0 else 0, x if last != 1 else 0, y if last != 2 else 0)
        step = (z if last == 0 else 0, x if last == 1 else 0, y if last == 2 else 0)
        from_ref = x_ref if held == (0, 0, 0) else slot(*source(*held), core)
        index = (z * nx + x) * nwa + y
        return pltpu.make_async_remote_copy(
            src_ref=from_ref, dst_ref=slot(*source(*held), core), send_sem=send_sem.at[index],
            recv_sem=recv_sem.at[index], device_id=device(*target(*step), core), device_id_type=MESH)

    def across(z, x, y):
        from_ref = x_ref if (z, x, y) == (0, 0, 0) else slot(*source(z, x, y), core)
        index = (z * nx + x) * nwa + y
        return pltpu.make_async_remote_copy(
            src_ref=from_ref, dst_ref=slot(*source(z, x, y), core), send_sem=fsend_sem.at[index],
            recv_sem=frecv_sem.at[index], device_id=device(pz, px, wa, 1 - core), device_id_type=MESH)

    def last_axis(z, x, y):
        if x == 0 and y == 0:
            return 0
        if x == 0 or y == 0:
            return 1 if y == 0 else 2
        return 2 if z % 2 == 0 else 1

    def onward(z, x, y):
        sends = []
        if (z, x, y) == (0, 0, 0):
            sends += [(q, 0, 0) for q in range(1, nz)]
        if x == 0 and y == 0:
            sends += [(z, q, 0) for q in range(1, nx)] + [(z, 0, q) for q in range(1, nwa)]
        elif y == 0 and z % 2 == 0:
            sends += [(z, x, q) for q in range(1, nwa)]
        elif x == 0 and z % 2 == 1:
            sends += [(z, q, y) for q in range(1, nx)]
        for place in sends:
            hop(*place, last_axis(*place)).start()
        across(z, x, y).start()

    places = [(z, x, y) for z in range(nz) for x in range(nx) for y in range(nwa)]
    places.sort(key=lambda place: (min(place[0], nz - place[0]) + place[1] + place[2], place))
    for place in places:
        if place != (0, 0, 0):
            hop(*place, last_axis(*place)).wait_recv()
        onward(*place)

    cond_ref[...] = jnp.zeros_like(cond_ref)
    row0 = pl.multiple_of(wa * nrows, nrows)
    own.wait()
    for place in places:
        across(*place).wait_recv()

    kk_count = klocal // g
    per = LANES // pts
    kpad = tri_ref.shape[0] // n
    lane_group = lax.broadcasted_iota(jnp.int32, (slots.shape[1], LANES), 1) // pts

    def unpack(t, carry):
        w, tile = t // (npb // per), lax.rem(t, npb // per)
        blocks = [slots[t * per + i].astype(F32) for i in range(per)]
        at = pl.ds(pl.multiple_of(tile * LANES, LANES), LANES)
        for i in range(per):
            base = kk_count * (nval + ncond)
            tri_ref[pl.ds((t * per + i) * kpad, klocal), :] = blocks[i][base:base + klocal]
        for j in range(g):
            whole = None
            for i in range(per):
                shift = (i - j) * pts % LANES
                moved = pltpu.roll(blocks[i], shift, 1) if shift else blocks[i]
                whole = moved if whole is None else jnp.where(lane_group == i, moved, whole)
            for kk in range(kk_count):
                k = w * klocal + j * kk_count + kk
                val_ref[k, :, at] = whole[kk * nval:(kk + 1) * nval]
                base = kk_count * nval + kk * ncond
                cond_ref[k, 0:ncond, at] = whole[base:base + ncond]
        return carry

    lax.fori_loop(0, n // per, unpack, 0)
    condb_ref[...] = cond_ref[...].astype(BF16)

    def inverse(k):
        found = jnp.int32(0)
        for j in range(kcount):
            found = jnp.where(kmap_ref[j] == k, j, found)
        return found

    pairs = nval * nval
    block = math.gcd(kcount, max(1, 256 // pairs))
    spread = nval // r

    def one_y(k, carry):
        w, kl = k // klocal, lax.rem(k, klocal)
        rows = {}
        parts = []
        for u in range(nval):
            if u // r not in rows:
                start = (w * npb + u // r) * kpad + kl
                rows[u // r] = tri_ref[pl.ds(start, ntrial, stride=spread * kpad), :]
            shift = -(u % r) * ncond % LANES
            parts.append((pltpu.roll(rows[u // r], shift, 1) if shift else rows[u // r])[:, :crows])
        left = jnp.concatenate(parts, axis=0).astype(BF16)
        y_ref[k] = lax.dot_general(left, condb_ref[k], (((1,), (0,)), ((), ())), preferred_element_type=F32)
        return carry

    lax.fori_loop(0, kcount, one_y, 0)

    def build(b, pick, start, width):
        for i in range(block):
            k = b * block + i
            here = val_ref[k, :, pl.ds(start, width)]
            there = val_ref[pick(k), :, pl.ds(start, width)]
            for v in range(0, nval, 2):
                two = jnp.concatenate([here[v:v + 1] * there, here[v + 1:v + 2] * there], axis=0)
                a_ref[i * pairs + v * nval:i * pairs + (v + 2) * nval, 0:width] = two.astype(BF16)

    def first(b, carry):
        build(b, lambda k: kmap_ref[k], 0, points)
        out = lax.dot_general(a_ref[...], w_ref[...], (((1,), (1,)), ((), ())), preferred_element_type=F32)
        wa_ref[pl.ds(b * block, block)] = out.astype(BF16).astype(F32).reshape(block, pairs, nrows)
        return carry

    lax.fori_loop(0, kcount // block, first, 0)

    def second(b, carry):
        build(b, inverse, row0, nrows)
        out = lax.dot_general(a_ref[:, 0:nrows], w_ref[...], (((1,), (0,)), ((), ())), preferred_element_type=F32)
        aw_ref[pl.ds(b * block, block)] = out.reshape(block, pairs, points)
        return carry

    lax.fori_loop(0, kcount // block, second, 0)
    acc_ref[...] = jnp.zeros_like(acc_ref)
    chunk = math.gcd(nrows, LANES)

    def combine(k, weight_ref, other, start, base, width):
        for c in range(0, width, chunk):
            at = pl.ds(pl.multiple_of(start + c, chunk), chunk)
            ys = [y_ref[other, u * ntrial:(u + 1) * ntrial, at] for u in range(nval)]
            for v in range(nval):
                total = None
                for u in range(nval):
                    row = v * nval + u
                    term = weight_ref[k, row:row + 1, c:c + chunk] * ys[u]
                    total = term if total is None else total + term
                z_ref[v * ntrial:(v + 1) * ntrial, base + c:base + c + chunk] = total.astype(BF16)

    def one_k(k, carry):
        combine(k, wa_ref, kmap_ref[k], row0, 0, nrows)
        combine(k, aw_ref, inverse(k), 0, nrows, points)
        spot = lax.rem(k, klocal)
        both = jnp.concatenate([condb_ref[k, :, pl.ds(row0, nrows)], condb_ref[k]], axis=1)
        wide = jnp.concatenate(
            [both * jnp.where(spot == j, 1.0, 0.0).astype(BF16) for j in range(klocal)], axis=0)
        acc_ref[k // klocal] += lax.dot_general(
            z_ref[...], wide, (((1,), (1,)), ((), ())), preferred_element_type=F32)
        return carry

    def give(w, i):
        return pltpu.make_async_remote_copy(
            src_ref=part_ref.at[w * npb + i], dst_ref=rslots.at[me], send_sem=rsend_sem.at[w * npb + i],
            recv_sem=rrecv_sem.at[me], device_id=(i, w), device_id_type=MESH)

    for w in range(nwa):
        lax.fori_loop(w * klocal, (w + 1) * klocal, one_k, 0)
        for i in range(npb):
            s, v0 = i * r // nval, i * r % nval
            part_ref[w * npb + i] = acc_ref[w, pl.ds(v0 * ntrial + s, r, stride=ntrial), :]

        def send(i, carry, w=w):
            to = lax.rem(pb + i, npb)

            @pl.when(jnp.logical_or(to != pb, wa != w))
            def go():
                give(w, to).start()
            return carry

        lax.fori_loop(0, npb, send, 0)

    def receive(j, carry):
        t = lax.rem(me + j, n)
        pltpu.make_async_remote_copy(
            src_ref=part_ref.at[t], dst_ref=rslots.at[t], send_sem=rsend_sem.at[t],
            recv_sem=rrecv_sem.at[t], device_id=(lax.rem(t, npb), t // npb), device_id_type=MESH).wait_recv()
        return carry

    lax.fori_loop(1, n, receive, 0)
    total = part_ref[me]

    def add(j, total):
        return total + rslots[lax.rem(me + j, n)]

    out_ref[...] = lax.fori_loop(1, n, add, total)

    def finish(j, carry):
        t = lax.rem(me + j, n)
        give(t // npb, lax.rem(t, npb)).wait_send()
        return carry

    lax.fori_loop(1, n, finish, 0)
    for place in places:
        if place != (0, 0, 0):
            hop(*place, last_axis(*place)).wait_send()
        across(*place).wait_send()


def shards(npb, nwa, psi_val, psi_cond, trials, screened, kmap):
    klocal, nval, pts = psi_val.shape
    ncond = psi_cond.shape[1]
    cols = trials.shape[1]
    kcount, points, n = klocal * nwa, pts * npb, npb * nwa
    ntrial = cols * npb // (nval * ncond)
    weights = screened[0]
    nrows = weights.shape[0]
    vmem = pl.BlockSpec(memory_space=pltpu.VMEM)
    smem = pl.BlockSpec(memory_space=pltpu.SMEM)
    g = math.gcd(klocal, LANES // pts)
    kk = klocal // g

    def lanes(a):
        a = a.reshape(g, kk * a.shape[1], pts)
        a = jnp.concatenate([a[j] for j in range(g)], axis=1)
        return jnp.pad(a, ((0, 0), (0, LANES - a.shape[1])))

    rows = kk * (nval + ncond) + klocal
    prow = up(rows, PACK)
    packed = jnp.concatenate(
        [lanes(psi_val), lanes(psi_cond), jnp.pad(trials, ((0, prow - rows), (0, LANES - cols)))], axis=0)
    r = cols // ncond
    crows = up(ncond, PACK)
    width = klocal * crows
    pairs = nval * nval
    block = math.gcd(kcount, max(1, 256 // pairs))
    dims = (npb, nwa, klocal, nval, ncond, pts, ntrial, nrows, g, r)
    dma = pltpu.SemaphoreType.DMA
    mine = pl.pallas_call(
        functools.partial(kernel, dims),
        out_shape=jax.ShapeDtypeStruct((r, width), F32),
        in_specs=[smem, vmem, vmem], out_specs=vmem,
        scratch_shapes=[
            pltpu.VMEM((n, prow, LANES), BF16),
            pltpu.VMEM((kcount, nval, points), F32),
            pltpu.VMEM((kcount, crows, points), F32),
            pltpu.VMEM((kcount, crows, points), BF16),
            pltpu.VMEM((n * up(klocal, 8), LANES), F32),
            pltpu.VMEM((block * pairs, points), BF16),
            pltpu.VMEM((kcount, pairs, nrows), F32),
            pltpu.VMEM((kcount, pairs, points), F32),
            pltpu.VMEM((kcount, nval * ntrial, points), F32),
            pltpu.VMEM((nval * ntrial, nrows + points), BF16),
            pltpu.VMEM((nwa, nval * ntrial, width), F32),
            pltpu.VMEM((n, r, width), F32),
            pltpu.VMEM((n, r, width), F32),
            dma, dma((n // 2,)), dma((n // 2,)), dma((n // 2,)), dma((n // 2,)), dma((n,)), dma((n,)),
        ],
        compiler_params=pltpu.CompilerParams(collective_id=0, has_side_effects=True),
        name="bethe",
    )(kmap[0], packed, weights)
    mine = mine.reshape(r, klocal, crows)[:, :, :ncond]
    return mine.transpose(1, 0, 2).reshape(klocal, cols)


def solution(mesh):
    in_specs = (
        P("wa", None, "pb"),
        P("wa", None, "pb"),
        P("wa", "pb"),
        P("pb", "wa", None),
        P("pb", None),
    )
    body = functools.partial(shards, mesh.shape["pb"], mesh.shape["wa"])
    return jax.shard_map(body, mesh=mesh, in_specs=in_specs, out_specs=P("wa", "pb"), check_vma=False)
```

```python
import functools
import math

import jax
import jax.numpy as jnp
from jax import lax
from jax.experimental import pallas as pl
from jax.experimental.pallas import tpu as pltpu
from jax.sharding import PartitionSpec as P

MESH = pl.DeviceIdType.MESH
LANES = 128
PACK = 16
F32 = jnp.float32
BF16 = jnp.bfloat16


def up(value, unit):
    return -(-value // unit) * unit


def kernel(dims, kmap_ref, x_ref, w_ref, out_ref, slots, val_ref, cond_ref, condb_ref, tri_ref,
           a_ref, wa_ref, aw_ref, y_ref, z_ref, acc_ref, part_ref, rslots,
           own_sem, send_sem, recv_sem, fsend_sem, frecv_sem, rsend_sem, rrecv_sem):
    npb, nwa, klocal, nval, ncond, pts, ntrial, nrows, g, r = dims
    kcount, points, n = klocal * nwa, pts * npb, npb * nwa
    crows = condb_ref.shape[1]
    pb, wa = lax.axis_index("pb"), lax.axis_index("wa")
    me = wa * npb + pb
    nx = 2 if npb % 4 == 0 else 1
    nz = npb // (2 * nx)
    core, px, pz = lax.rem(pb, 2), lax.rem(pb // 2, nx), pb // (2 * nx)

    def device(z, x, y, c):
        return (z * nx + x) * 2 + c, y

    def source(z, x, y):
        return (lax.rem(pz - z + nz, nz), lax.rem(px - x + nx, nx), lax.rem(wa - y + nwa, nwa))

    def target(z, x, y):
        return (lax.rem(pz + z, nz), lax.rem(px + x, nx), lax.rem(wa + y, nwa))

    def slot(z, x, y, c):
        p, w = device(z, x, y, c)
        return slots.at[w * npb + p]

    barrier = pltpu.get_barrier_semaphore()

    def greet(j, carry):
        t = lax.rem(me + j, n)
        pl.semaphore_signal(barrier, inc=1, device_id=(lax.rem(t, npb), t // npb), device_id_type=MESH)
        return carry

    lax.fori_loop(1, n, greet, 0)
    own = pltpu.make_async_copy(x_ref, slots.at[me], own_sem)
    own.start()
    pl.semaphore_wait(barrier, n - 1)

    def hop(z, x, y, last):
        held = (z if last != 0 else 0, x if last != 1 else 0, y if last != 2 else 0)
        step = (z if last == 0 else 0, x if last == 1 else 0, y if last == 2 else 0)
        from_ref = x_ref if held == (0, 0, 0) else slot(*source(*held), core)
        index = (z * nx + x) * nwa + y
        return pltpu.make_async_remote_copy(
            src_ref=from_ref, dst_ref=slot(*source(*held), core), send_sem=send_sem.at[index],
            recv_sem=recv_sem.at[index], device_id=device(*target(*step), core), device_id_type=MESH)

    def across(z, x, y):
        from_ref = x_ref if (z, x, y) == (0, 0, 0) else slot(*source(z, x, y), core)
        index = (z * nx + x) * nwa + y
        return pltpu.make_async_remote_copy(
            src_ref=from_ref, dst_ref=slot(*source(z, x, y), core), send_sem=fsend_sem.at[index],
            recv_sem=frecv_sem.at[index], device_id=device(pz, px, wa, 1 - core), device_id_type=MESH)

    def last_axis(z, x, y):
        if x == 0 and y == 0:
            return 0
        if x == 0 or y == 0:
            return 1 if y == 0 else 2
        return 2 if z % 2 == 0 else 1

    def onward(z, x, y):
        sends = []
        if (z, x, y) == (0, 0, 0):
            sends += [(q, 0, 0) for q in range(1, nz)]
        if x == 0 and y == 0:
            sends += [(z, q, 0) for q in range(1, nx)] + [(z, 0, q) for q in range(1, nwa)]
        elif y == 0 and z % 2 == 0:
            sends += [(z, x, q) for q in range(1, nwa)]
        elif x == 0 and z % 2 == 1:
            sends += [(z, q, y) for q in range(1, nx)]
        for place in sends:
            hop(*place, last_axis(*place)).start()
        across(z, x, y).start()

    places = [(z, x, y) for z in range(nz) for x in range(nx) for y in range(nwa)]
    places.sort(key=lambda place: (min(place[0], nz - place[0]) + place[1] + place[2], place))
    for place in places:
        if place != (0, 0, 0):
            hop(*place, last_axis(*place)).wait_recv()
        onward(*place)

    cond_ref[...] = jnp.zeros_like(cond_ref)
    row0 = pl.multiple_of(wa * nrows, nrows)
    own.wait()
    for place in places:
        across(*place).wait_recv()

    kk_count = klocal // g
    per = LANES // pts
    kpad = tri_ref.shape[0] // n
    lane_group = lax.broadcasted_iota(jnp.int32, (slots.shape[1], LANES), 1) // pts

    def unpack(t, carry):
        w, tile = t // (npb // per), lax.rem(t, npb // per)
        blocks = [slots[t * per + i].astype(F32) for i in range(per)]
        at = pl.ds(pl.multiple_of(tile * LANES, LANES), LANES)
        for i in range(per):
            base = kk_count * (nval + ncond)
            tri_ref[pl.ds((t * per + i) * kpad, klocal), :] = blocks[i][base:base + klocal]
        for j in range(g):
            whole = None
            for i in range(per):
                shift = (i - j) * pts % LANES
                moved = pltpu.roll(blocks[i], shift, 1) if shift else blocks[i]
                whole = moved if whole is None else jnp.where(lane_group == i, moved, whole)
            for kk in range(kk_count):
                k = w * klocal + j * kk_count + kk
                val_ref[k, :, at] = whole[kk * nval:(kk + 1) * nval]
                base = kk_count * nval + kk * ncond
                cond_ref[k, 0:ncond, at] = whole[base:base + ncond]
        return carry

    lax.fori_loop(0, n // per, unpack, 0)
    condb_ref[...] = cond_ref[...].astype(BF16)

    def inverse(k):
        found = jnp.int32(0)
        for j in range(kcount):
            found = jnp.where(kmap_ref[j] == k, j, found)
        return found

    pairs = nval * nval
    block = math.gcd(kcount, max(1, 256 // pairs))
    spread = nval // r

    def one_y(k, carry):
        w, kl = k // klocal, lax.rem(k, klocal)
        rows = {}
        parts = []
        for u in range(nval):
            if u // r not in rows:
                start = (w * npb + u // r) * kpad + kl
                rows[u // r] = tri_ref[pl.ds(start, ntrial, stride=spread * kpad), :]
            shift = -(u % r) * ncond % LANES
            parts.append((pltpu.roll(rows[u // r], shift, 1) if shift else rows[u // r])[:, :crows])
        left = jnp.concatenate(parts, axis=0).astype(BF16)
        y_ref[k] = lax.dot_general(left, condb_ref[k], (((1,), (0,)), ((), ())), preferred_element_type=F32)
        return carry

    lax.fori_loop(0, kcount, one_y, 0, unroll=math.gcd(kcount, 4))

    def build(half, b, pick, start, width):
        for i in range(block):
            k = b * block + i
            here = val_ref[k, :, pl.ds(start, width)]
            there = val_ref[pick(k), :, pl.ds(start, width)]
            for v in range(0, nval, 2):
                two = jnp.concatenate([here[v:v + 1] * there, here[v + 1:v + 2] * there], axis=0)
                a_ref[half, i * pairs + v * nval:i * pairs + (v + 2) * nval, 0:width] = two.astype(BF16)

    def first(step, carry):
        for half in range(halves):
            b = step * halves + half
            build(half, b, lambda k: kmap_ref[k], 0, points)
            out = lax.dot_general(a_ref[half], w_ref[...], (((1,), (1,)), ((), ())), preferred_element_type=F32)
            wa_ref[pl.ds(b * block, block)] = out.astype(BF16).astype(F32).reshape(block, pairs, nrows)
        return carry

    halves = a_ref.shape[0]
    lax.fori_loop(0, kcount // block // halves, first, 0)

    def second(step, carry):
        for half in range(halves):
            b = step * halves + half
            build(half, b, inverse, row0, nrows)
            out = lax.dot_general(a_ref[half, :, 0:nrows], w_ref[...], (((1,), (0,)), ((), ())), preferred_element_type=F32)
            aw_ref[pl.ds(b * block, block)] = out.reshape(block, pairs, points)
        return carry

    lax.fori_loop(0, kcount // block // halves, second, 0)
    acc_ref[...] = jnp.zeros_like(acc_ref)
    chunk = math.gcd(nrows, LANES)
    group = z_ref.shape[0]

    def combine(i, k, weight_ref, other, start, base, width):
        for c in range(0, width, chunk):
            at = pl.ds(pl.multiple_of(start + c, chunk), chunk)
            ys = [y_ref[other, u * ntrial:(u + 1) * ntrial, at] for u in range(nval)]
            for v in range(nval):
                total = None
                for u in range(nval):
                    row = v * nval + u
                    term = weight_ref[k, row:row + 1, c:c + chunk] * ys[u]
                    total = term if total is None else total + term
                z_ref[i, v * ntrial:(v + 1) * ntrial, base + c:base + c + chunk] = total.astype(BF16)

    def some_k(step, carry):
        total = None
        for i in range(group):
            k = step * group + i
            combine(i, k, wa_ref, kmap_ref[k], row0, 0, nrows)
            combine(i, k, aw_ref, inverse(k), 0, nrows, points)
            spot = lax.rem(k, klocal)
            both = jnp.concatenate([condb_ref[k, :, pl.ds(row0, nrows)], condb_ref[k]], axis=1)
            wide = jnp.concatenate(
                [both * jnp.where(spot == j, 1.0, 0.0).astype(BF16) for j in range(klocal)], axis=0)
            term = lax.dot_general(z_ref[i], wide, (((1,), (1,)), ((), ())), preferred_element_type=F32)
            total = term if total is None else total + term
        acc_ref[step * group // klocal] += total
        return carry

    def give(w, i):
        return pltpu.make_async_remote_copy(
            src_ref=part_ref.at[w * npb + i], dst_ref=rslots.at[me], send_sem=rsend_sem.at[w * npb + i],
            recv_sem=rrecv_sem.at[me], device_id=(i, w), device_id_type=MESH)

    for w in range(nwa):
        lax.fori_loop(w * klocal // group, (w + 1) * klocal // group, some_k, 0)
        for i in range(npb):
            s, v0 = i * r // nval, i * r % nval
            part_ref[w * npb + i] = acc_ref[w, pl.ds(v0 * ntrial + s, r, stride=ntrial), :]

        def send(i, carry, w=w):
            to = lax.rem(pb + i, npb)

            @pl.when(jnp.logical_or(to != pb, wa != w))
            def go():
                give(w, to).start()
            return carry

        lax.fori_loop(0, npb, send, 0)

    def receive(j, carry):
        t = lax.rem(me + j, n)
        pltpu.make_async_remote_copy(
            src_ref=part_ref.at[t], dst_ref=rslots.at[t], send_sem=rsend_sem.at[t],
            recv_sem=rrecv_sem.at[t], device_id=(lax.rem(t, npb), t // npb), device_id_type=MESH).wait_recv()
        return carry

    lax.fori_loop(1, n, receive, 0)
    total = part_ref[me]

    def add(j, total):
        return total + rslots[lax.rem(me + j, n)]

    out_ref[...] = lax.fori_loop(1, n, add, total)

    def finish(j, carry):
        t = lax.rem(me + j, n)
        give(t // npb, lax.rem(t, npb)).wait_send()
        return carry

    lax.fori_loop(1, n, finish, 0)
    for place in places:
        if place != (0, 0, 0):
            hop(*place, last_axis(*place)).wait_send()
        across(*place).wait_send()


def shards(npb, nwa, psi_val, psi_cond, trials, screened, kmap):
    klocal, nval, pts = psi_val.shape
    ncond = psi_cond.shape[1]
    cols = trials.shape[1]
    kcount, points, n = klocal * nwa, pts * npb, npb * nwa
    ntrial = cols * npb // (nval * ncond)
    weights = screened[0]
    nrows = weights.shape[0]
    vmem = pl.BlockSpec(memory_space=pltpu.VMEM)
    smem = pl.BlockSpec(memory_space=pltpu.SMEM)
    g = math.gcd(klocal, LANES // pts)
    kk = klocal // g

    def lanes(a):
        a = a.reshape(g, kk * a.shape[1], pts)
        a = jnp.concatenate([a[j] for j in range(g)], axis=1)
        return jnp.pad(a, ((0, 0), (0, LANES - a.shape[1])))

    rows = kk * (nval + ncond) + klocal
    prow = up(rows, PACK)
    packed = jnp.concatenate(
        [lanes(psi_val), lanes(psi_cond), jnp.pad(trials, ((0, prow - rows), (0, LANES - cols)))], axis=0)
    r = cols // ncond
    crows = up(ncond, PACK)
    width = klocal * crows
    pairs = nval * nval
    block = math.gcd(kcount, max(1, 256 // pairs))
    dims = (npb, nwa, klocal, nval, ncond, pts, ntrial, nrows, g, r)
    dma = pltpu.SemaphoreType.DMA
    mine = pl.pallas_call(
        functools.partial(kernel, dims),
        out_shape=jax.ShapeDtypeStruct((r, width), F32),
        in_specs=[smem, vmem, vmem], out_specs=vmem,
        scratch_shapes=[
            pltpu.VMEM((n, prow, LANES), BF16),
            pltpu.VMEM((kcount, nval, points), F32),
            pltpu.VMEM((kcount, crows, points), F32),
            pltpu.VMEM((kcount, crows, points), BF16),
            pltpu.VMEM((n * up(klocal, 8), LANES), F32),
            pltpu.VMEM((math.gcd(kcount // block, 2), block * pairs, points), BF16),
            pltpu.VMEM((kcount, pairs, nrows), F32),
            pltpu.VMEM((kcount, pairs, points), F32),
            pltpu.VMEM((kcount, nval * ntrial, points), F32),
            pltpu.VMEM((math.gcd(klocal, 4), nval * ntrial, nrows + points), BF16),
            pltpu.VMEM((nwa, nval * ntrial, width), F32),
            pltpu.VMEM((n, r, width), F32),
            pltpu.VMEM((n, r, width), F32),
            dma, dma((n // 2,)), dma((n // 2,)), dma((n // 2,)), dma((n // 2,)), dma((n,)), dma((n,)),
        ],
        compiler_params=pltpu.CompilerParams(collective_id=0, has_side_effects=True),
        name="bethe",
    )(kmap[0], packed, weights)
    mine = mine.reshape(r, klocal, crows)[:, :, :ncond]
    return mine.transpose(1, 0, 2).reshape(klocal, cols)


def solution(mesh):
    in_specs = (
        P("wa", None, "pb"),
        P("wa", None, "pb"),
        P("wa", "pb"),
        P("pb", "wa", None),
        P("pb", None),
    )
    body = functools.partial(shards, mesh.shape["pb"], mesh.shape["wa"])
    return jax.shard_map(body, mesh=mesh, in_specs=in_specs, out_specs=P("wa", "pb"), check_vma=False)
```

```python
import functools
import math

import jax
import jax.numpy as jnp
from jax import lax
from jax.experimental import pallas as pl
from jax.experimental.pallas import tpu as pltpu
from jax.sharding import PartitionSpec as P

MESH = pl.DeviceIdType.MESH
LANES = 128
PACK = 16
F32 = jnp.float32
BF16 = jnp.bfloat16


def up(value, unit):
    return -(-value // unit) * unit


def kernel(dims, kmap_ref, x_ref, whbm_ref, out_ref, w_ref, w_sem, slots, val_ref, cond_ref, condb_ref, tri_ref,
           a_ref, wa_ref, aw_ref, y_ref, z_ref, acc_ref, part_ref, rslots,
           own_sem, send_sem, recv_sem, fsend_sem, frecv_sem, rsend_sem, rrecv_sem):
    npb, nwa, klocal, nval, ncond, pts, ntrial, nrows, g, r = dims
    kcount, points, n = klocal * nwa, pts * npb, npb * nwa
    crows = condb_ref.shape[1]
    pb, wa = lax.axis_index("pb"), lax.axis_index("wa")
    me = wa * npb + pb
    nx = 2 if npb % 4 == 0 else 1
    nz = npb // (2 * nx)
    core, px, pz = lax.rem(pb, 2), lax.rem(pb // 2, nx), pb // (2 * nx)

    def device(z, x, y, c):
        return (z * nx + x) * 2 + c, y

    def source(z, x, y):
        return (lax.rem(pz - z + nz, nz), lax.rem(px - x + nx, nx), lax.rem(wa - y + nwa, nwa))

    def target(z, x, y):
        return (lax.rem(pz + z, nz), lax.rem(px + x, nx), lax.rem(wa + y, nwa))

    def slot(z, x, y, c):
        p, w = device(z, x, y, c)
        return slots.at[w * npb + p]

    barrier = pltpu.get_barrier_semaphore()

    def greet(j, carry):
        t = lax.rem(me + j, n)
        pl.semaphore_signal(barrier, inc=1, device_id=(lax.rem(t, npb), t // npb), device_id_type=MESH)
        return carry

    lax.fori_loop(1, n, greet, 0)
    own = pltpu.make_async_copy(x_ref, slots.at[me], own_sem)
    own.start()
    load = pltpu.make_async_copy(whbm_ref.at[0], w_ref, w_sem)
    load.start()
    cond_ref[...] = jnp.zeros_like(cond_ref)
    acc_ref[...] = jnp.zeros_like(acc_ref)
    own.wait()
    pl.semaphore_wait(barrier, n - 1)

    def hop(z, x, y, last):
        held = (z if last != 0 else 0, x if last != 1 else 0, y if last != 2 else 0)
        step = (z if last == 0 else 0, x if last == 1 else 0, y if last == 2 else 0)
        from_ref = x_ref if held == (0, 0, 0) else slot(*source(*held), core)
        index = (z * nx + x) * nwa + y
        return pltpu.make_async_remote_copy(
            src_ref=from_ref, dst_ref=slot(*source(*held), core), send_sem=send_sem.at[index],
            recv_sem=recv_sem.at[index], device_id=device(*target(*step), core), device_id_type=MESH)

    def across(z, x, y):
        from_ref = x_ref if (z, x, y) == (0, 0, 0) else slot(*source(z, x, y), core)
        index = (z * nx + x) * nwa + y
        return pltpu.make_async_remote_copy(
            src_ref=from_ref, dst_ref=slot(*source(z, x, y), core), send_sem=fsend_sem.at[index],
            recv_sem=frecv_sem.at[index], device_id=device(pz, px, wa, 1 - core), device_id_type=MESH)

    def last_axis(z, x, y):
        if x == 0 and y == 0:
            return 0
        if x == 0 or y == 0:
            return 1 if y == 0 else 2
        return 2 if z % 2 == 0 else 1

    def onward(z, x, y):
        sends = []
        if (z, x, y) == (0, 0, 0):
            sends += [(q, 0, 0) for q in range(1, nz)]
        if x == 0 and y == 0:
            sends += [(z, q, 0) for q in range(1, nx)] + [(z, 0, q) for q in range(1, nwa)]
        elif y == 0 and z % 2 == 0:
            sends += [(z, x, q) for q in range(1, nwa)]
        elif x == 0 and z % 2 == 1:
            sends += [(z, q, y) for q in range(1, nx)]
        for place in sends:
            hop(*place, last_axis(*place)).start()
        across(z, x, y).start()

    places = [(z, x, y) for z in range(nz) for x in range(nx) for y in range(nwa)]
    places.sort(key=lambda place: (min(place[0], nz - place[0]) + place[1] + place[2], place))
    row0 = pl.multiple_of(wa * nrows, nrows)

    kk_count = klocal // g
    per = LANES // pts
    kpad = tri_ref.shape[0] // n
    lane_group = lax.broadcasted_iota(jnp.int32, (slots.shape[1], LANES), 1) // pts

    def unpack(t, carry):
        w, tile = t // (npb // per), lax.rem(t, npb // per)
        blocks = [slots[t * per + i].astype(F32) for i in range(per)]
        at = pl.ds(pl.multiple_of(tile * LANES, LANES), LANES)
        for i in range(per):
            base = kk_count * (nval + ncond)
            tri_ref[pl.ds((t * per + i) * kpad, klocal), :] = blocks[i][base:base + klocal]
        for j in range(g):
            whole = None
            for i in range(per):
                shift = (i - j) * pts % LANES
                moved = pltpu.roll(blocks[i], shift, 1) if shift else blocks[i]
                whole = moved if whole is None else jnp.where(lane_group == i, moved, whole)
            for kk in range(kk_count):
                k = w * klocal + j * kk_count + kk
                val_ref[k, :, at] = whole[kk * nval:(kk + 1) * nval]
                base = kk_count * nval + kk * ncond
                cond_ref[k, 0:ncond, at] = whole[base:base + ncond]
        return carry

    early = per == 2
    lag = 3

    def collect(place):
        across(*place).wait_recv()
        if early:
            z, x, y = source(*place)
            unpack(y * (npb // 2) + z * nx + x, 0)

    for number, place in enumerate(places):
        if place != (0, 0, 0):
            hop(*place, last_axis(*place)).wait_recv()
        onward(*place)
        if number >= lag:
            collect(places[number - lag])
    for place in places[-lag:] if len(places) >= lag else places:
        collect(place)
    if not early:
        lax.fori_loop(0, n // per, unpack, 0)
    condb_ref[...] = cond_ref[...].astype(BF16)

    def inverse(k):
        found = jnp.int32(0)
        for j in range(kcount):
            found = jnp.where(kmap_ref[j] == k, j, found)
        return found

    pairs = nval * nval
    block = math.gcd(kcount, max(1, 256 // pairs))
    spread = nval // r

    def one_y(k, carry):
        w, kl = k // klocal, lax.rem(k, klocal)
        rows = {}
        parts = []
        for u in range(nval):
            if u // r not in rows:
                start = (w * npb + u // r) * kpad + kl
                rows[u // r] = tri_ref[pl.ds(start, ntrial, stride=spread * kpad), :]
            shift = -(u % r) * ncond % LANES
            parts.append((pltpu.roll(rows[u // r], shift, 1) if shift else rows[u // r])[:, :crows])
        left = jnp.concatenate(parts, axis=0).astype(BF16)
        y_ref[k] = lax.dot_general(left, condb_ref[k], (((1,), (0,)), ((), ())), preferred_element_type=F32)
        return carry

    lax.fori_loop(0, kcount, one_y, 0, unroll=math.gcd(kcount, 4))

    def build(half, b, pick, start, width):
        for i in range(block):
            k = b * block + i
            here = val_ref[k, :, pl.ds(start, width)]
            there = val_ref[pick(k), :, pl.ds(start, width)]
            for v in range(0, nval, 2):
                two = jnp.concatenate([here[v:v + 1] * there, here[v + 1:v + 2] * there], axis=0)
                a_ref[half, i * pairs + v * nval:i * pairs + (v + 2) * nval, 0:width] = two.astype(BF16)

    load.wait()

    def first(step, carry):
        for half in range(halves):
            b = step * halves + half
            build(half, b, lambda k: kmap_ref[k], 0, points)
            out = lax.dot_general(a_ref[half], w_ref[...], (((1,), (1,)), ((), ())), preferred_element_type=F32)
            wa_ref[pl.ds(b * block, block)] = out.astype(BF16).astype(F32).reshape(block, pairs, nrows)
        return carry

    halves = a_ref.shape[0]
    lax.fori_loop(0, kcount // block // halves, first, 0)

    def second(step, carry):
        for half in range(halves):
            b = step * halves + half
            build(half, b, inverse, row0, nrows)
            out = lax.dot_general(a_ref[half, :, 0:nrows], w_ref[...], (((1,), (0,)), ((), ())), preferred_element_type=F32)
            aw_ref[pl.ds(b * block, block)] = out.reshape(block, pairs, points)
        return carry

    lax.fori_loop(0, kcount // block // halves, second, 0)
    chunk = math.gcd(nrows, LANES)
    group = z_ref.shape[0]

    def combine(i, k, weight_ref, other, start, base, width):
        for c in range(0, width, chunk):
            at = pl.ds(pl.multiple_of(start + c, chunk), chunk)
            ys = [y_ref[other, u * ntrial:(u + 1) * ntrial, at] for u in range(nval)]
            for v in range(nval):
                total = None
                for u in range(nval):
                    row = v * nval + u
                    term = weight_ref[k, row:row + 1, c:c + chunk] * ys[u]
                    total = term if total is None else total + term
                z_ref[i, v * ntrial:(v + 1) * ntrial, base + c:base + c + chunk] = total.astype(BF16)

    def some_k(step, carry):
        total = None
        for i in range(group):
            k = step * group + i
            combine(i, k, wa_ref, kmap_ref[k], row0, 0, nrows)
            combine(i, k, aw_ref, inverse(k), 0, nrows, points)
            spot = lax.rem(k, klocal)
            both = jnp.concatenate([condb_ref[k, :, pl.ds(row0, nrows)], condb_ref[k]], axis=1)
            wide = jnp.concatenate(
                [both * jnp.where(spot == j, 1.0, 0.0).astype(BF16) for j in range(klocal)], axis=0)
            term = lax.dot_general(z_ref[i], wide, (((1,), (1,)), ((), ())), preferred_element_type=F32)
            total = term if total is None else total + term
        acc_ref[step * group // klocal] += total
        return carry

    def give(w, i):
        return pltpu.make_async_remote_copy(
            src_ref=part_ref.at[w * npb + i], dst_ref=rslots.at[me], send_sem=rsend_sem.at[w * npb + i],
            recv_sem=rrecv_sem.at[me], device_id=(i, w), device_id_type=MESH)

    for w in range(nwa):
        lax.fori_loop(w * klocal // group, (w + 1) * klocal // group, some_k, 0)
        for i in range(npb):
            s, v0 = i * r // nval, i * r % nval
            part_ref[w * npb + i] = acc_ref[w, pl.ds(v0 * ntrial + s, r, stride=ntrial), :]

        def send(i, carry, w=w):
            to = lax.rem(pb + i, npb)

            @pl.when(jnp.logical_or(to != pb, wa != w))
            def go():
                give(w, to).start()
            return carry

        lax.fori_loop(0, npb, send, 0)

    def receive(j, carry):
        t = lax.rem(me + j, n)
        pltpu.make_async_remote_copy(
            src_ref=part_ref.at[t], dst_ref=rslots.at[t], send_sem=rsend_sem.at[t],
            recv_sem=rrecv_sem.at[t], device_id=(lax.rem(t, npb), t // npb), device_id_type=MESH).wait_recv()
        return carry

    lax.fori_loop(1, n, receive, 0)
    total = part_ref[me]

    def add(j, total):
        return total + rslots[lax.rem(me + j, n)]

    out_ref[...] = lax.fori_loop(1, n, add, total)

    def finish(j, carry):
        t = lax.rem(me + j, n)
        give(t // npb, lax.rem(t, npb)).wait_send()
        return carry

    lax.fori_loop(1, n, finish, 0)
    for place in places:
        if place != (0, 0, 0):
            hop(*place, last_axis(*place)).wait_send()
        across(*place).wait_send()


def shards(npb, nwa, psi_val, psi_cond, trials, screened, kmap):
    klocal, nval, pts = psi_val.shape
    ncond = psi_cond.shape[1]
    cols = trials.shape[1]
    kcount, points, n = klocal * nwa, pts * npb, npb * nwa
    ntrial = cols * npb // (nval * ncond)
    nrows = screened.shape[1]
    vmem = pl.BlockSpec(memory_space=pltpu.VMEM)
    smem = pl.BlockSpec(memory_space=pltpu.SMEM)
    g = math.gcd(klocal, LANES // pts)
    kk = klocal // g

    def lanes(a):
        a = a.reshape(g, kk * a.shape[1], pts)
        a = jnp.concatenate([a[j] for j in range(g)], axis=1)
        return jnp.pad(a, ((0, 0), (0, LANES - a.shape[1])))

    rows = kk * (nval + ncond) + klocal
    prow = up(rows, PACK)
    packed = jnp.concatenate(
        [lanes(psi_val), lanes(psi_cond), jnp.pad(trials, ((0, prow - rows), (0, LANES - cols)))], axis=0)
    r = cols // ncond
    crows = up(ncond, PACK)
    width = klocal * crows
    pairs = nval * nval
    block = math.gcd(kcount, max(1, 256 // pairs))
    dims = (npb, nwa, klocal, nval, ncond, pts, ntrial, nrows, g, r)
    dma = pltpu.SemaphoreType.DMA
    mine = pl.pallas_call(
        functools.partial(kernel, dims),
        out_shape=jax.ShapeDtypeStruct((r, width), F32),
        in_specs=[smem, vmem, pl.BlockSpec(memory_space=pl.ANY)], out_specs=vmem,
        scratch_shapes=[
            pltpu.VMEM((nrows, points), BF16),
            dma,
            pltpu.VMEM((n, prow, LANES), BF16),
            pltpu.VMEM((kcount, nval, points), F32),
            pltpu.VMEM((kcount, crows, points), F32),
            pltpu.VMEM((kcount, crows, points), BF16),
            pltpu.VMEM((n * up(klocal, 8), LANES), F32),
            pltpu.VMEM((math.gcd(kcount // block, 2), block * pairs, points), BF16),
            pltpu.VMEM((kcount, pairs, nrows), F32),
            pltpu.VMEM((kcount, pairs, points), F32),
            pltpu.VMEM((kcount, nval * ntrial, points), F32),
            pltpu.VMEM((math.gcd(klocal, 4), nval * ntrial, nrows + points), BF16),
            pltpu.VMEM((nwa, nval * ntrial, width), F32),
            pltpu.VMEM((n, r, width), F32),
            pltpu.VMEM((n, r, width), F32),
            dma, dma((n // 2,)), dma((n // 2,)), dma((n // 2,)), dma((n // 2,)), dma((n,)), dma((n,)),
        ],
        compiler_params=pltpu.CompilerParams(collective_id=0, has_side_effects=True),
        name="bethe",
    )(kmap[0], packed, screened)
    mine = mine.reshape(r, klocal, crows)[:, :, :ncond]
    return mine.transpose(1, 0, 2).reshape(klocal, cols)


def solution(mesh):
    in_specs = (
        P("wa", None, "pb"),
        P("wa", None, "pb"),
        P("wa", "pb"),
        P("pb", "wa", None),
        P("pb", None),
    )
    body = functools.partial(shards, mesh.shape["pb"], mesh.shape["wa"])
    return jax.shard_map(body, mesh=mesh, in_specs=in_specs, out_specs=P("wa", "pb"), check_vma=False)
```
